256 devices in a mesh: grp: 8 (over x, core), seq: 32 (over y, z).
Axes of the slice: x: 4, y: 4, z: 8, core: 2. Of those that a mesh axis runs over, the one named last changes fastest.
Arguments:
- query_rows: bfloat16 [8, 2, 2560, 4096], P('grp', None, 'seq'), may hold values from -5 to 5
- key_rows: bfloat16 [8, 2, 2560, 4096], P('grp', None, 'seq'), may hold values from -5 to 5
- value_rows: bfloat16 [8, 2, 2560, 4096], P('grp', None, 'seq'), may hold values from -6 to 6
- out_grad: bfloat16 [8, 2, 2560, 4096], P('grp', None, 'seq'), may hold values from -6 to 6
- lengths: int32 [8, 2], replicated, may hold values from 512 to 2560, as said below
Outputs:
- attended: bfloat16 [8, 2, 2560, 4096], P('grp', None, 'seq')
- query_grad: bfloat16 [8, 2, 2560, 4096], P('grp', None, 'seq')
- key_grad: bfloat16 [8, 2, 2560, 4096], P('grp', None, 'seq')
- value_grad: bfloat16 [8, 2, 2560, 4096], P('grp', None, 'seq')
The draws below stay inside these ranges and needn't reach their ends.
Inputs may be any that keep to these rules, and one draw needn't show every extreme that they name: `lengths`: every length is a multiple of 128; in every draw some video has exactly 2560 tokens and some exactly 512.
All inputs are finite; a program needn't handle non-finite values.
Results may differ from the reference program's by a relative error of at most 0.02.
Values may be sent and summed in bfloat16 or wider, within the bound.
No kernel may reach another device: no remote copies, remote signals or barrier semaphores. Data moves between devices by JAX's collectives and lax.ppermute only.
A program may use at most 128 MiB of HBM per device.

```python
import jax
import jax.numpy as jnp
from jax import lax

HEADS = 32
HD = 128
MAX_LEN = 2560
MIN_LEN = 512
LEN_STEP = 128
PAIRS = 8
WIDTH = 4096


def draw_query_rows(key, part):
    base = jnp.clip(jax.random.normal(jax.random.fold_in(key, 1), (PAIRS, 2, MAX_LEN, WIDTH)), -4.0, 4.0)
    return base.astype(jnp.bfloat16)


def draw_key_rows(key, part):
    base = jnp.clip(jax.random.normal(jax.random.fold_in(key, 2), (PAIRS, 2, MAX_LEN, WIDTH)), -4.0, 4.0)
    return base.astype(jnp.bfloat16)


def draw_lengths(key, part):
    steps_low = MIN_LEN // LEN_STEP
    steps_high = MAX_LEN // LEN_STEP
    counts = jax.random.randint(jax.random.fold_in(key, 3), (PAIRS * 2,), steps_low, steps_high + 1)
    order = jax.random.permutation(jax.random.fold_in(key, 4), PAIRS * 2)
    counts = counts.at[order[0]].set(steps_high).at[order[1]].set(steps_low)
    return (counts * LEN_STEP).reshape(PAIRS, 2).astype(jnp.int32)


def levels(key, shape, cuts, low, high):
    level = 1.0
    for dim, blocks in cuts:
        steps = jax.random.uniform(jax.random.fold_in(jax.random.fold_in(key, 6), dim), (blocks,), jnp.float32, low / len(cuts), high / len(cuts))
        level = level * jnp.repeat(jnp.exp(steps), shape[dim] // blocks).reshape((-1,) + (1,) * (len(shape) - 1 - dim))
    return level


def gaussian(stream_key, extent, spread, most, cuts=(), kind=jnp.bfloat16):
    level = levels(stream_key, extent, cuts, -0.22, 0.18) if cuts else 1.0
    values = jax.random.normal(stream_key, extent, jnp.float32) * spread * level
    return jnp.minimum(jnp.maximum(values, -most), most).astype(kind)


def setup_inputs(seed: int = 0) -> dict:
    key_list = jax.random.split(jax.random.key(seed), 6)
    return {
        "query_rows": draw_query_rows(jax.random.fold_in(key_list[5], 71), 0),
        "key_rows": draw_key_rows(jax.random.fold_in(key_list[5], 71), 0),
        "value_rows": gaussian(key_list[2], (PAIRS, 2, MAX_LEN, WIDTH), 1.0, 6.0, ((0, 8), (2, 32))),
        "out_grad": gaussian(key_list[3], (PAIRS, 2, MAX_LEN, WIDTH), 1.0, 6.0, ((0, 8), (2, 32))),
        "lengths": draw_lengths(jax.random.fold_in(key_list[5], 71), 0),
    }


def head_pass(query, keys, values, grads, length):
    scaling = HD ** -0.5
    position = jnp.arange(MAX_LEN)
    is_valid = position < length
    scores = jnp.dot(query, keys.T, preferred_element_type=jnp.float32) * scaling
    scores = jnp.where(is_valid[None, :], scores, -1e30)
    largest = jnp.max(scores, axis=1, keepdims=True)
    weights = jnp.exp(scores - largest)
    probs = weights / jnp.sum(weights, axis=1, keepdims=True)
    probs = jnp.where(is_valid[:, None], probs, 0.0)
    probs_half = probs.astype(jnp.bfloat16)
    output = jnp.dot(probs_half, values, preferred_element_type=jnp.float32).astype(jnp.bfloat16)
    delta = jnp.sum(grads.astype(jnp.float32) * output.astype(jnp.float32), axis=1)
    grad_probs = jnp.dot(grads, values.T, preferred_element_type=jnp.float32)
    grad_scores = (probs * (grad_probs - delta[:, None])).astype(jnp.bfloat16)
    query_grad = (jnp.dot(grad_scores, keys, preferred_element_type=jnp.float32) * scaling).astype(jnp.bfloat16)
    key_grad = (jnp.dot(grad_scores.T, query, preferred_element_type=jnp.float32) * scaling).astype(jnp.bfloat16)
    value_grad = jnp.dot(probs_half.T, grads, preferred_element_type=jnp.float32).astype(jnp.bfloat16)
    return output, query_grad, key_grad, value_grad


def reference(query_rows, key_rows, value_rows, out_grad, lengths):
    results = ([], [], [], [])
    for pair_index in range(PAIRS):
        per_video = ([], [], [], [])
        for video in range(2):
            pieces = []
            for array in (query_rows, key_rows, value_rows, out_grad):
                block = array[pair_index, video]
                pieces.append(block.reshape(MAX_LEN, HEADS, HD).transpose(1, 0, 2))
            length = lengths[pair_index, video]
            outputs = lax.map(lambda item: head_pass(item[0], item[1], item[2], item[3], length), tuple(pieces))
            for number in range(4):
                per_video[number].append(outputs[number].transpose(1, 0, 2).reshape(MAX_LEN, HEADS * HD))
        for number in range(4):
            results[number].append(jnp.stack(per_video[number]))
    return (jnp.stack(results[0]), jnp.stack(results[1]), jnp.stack(results[2]), jnp.stack(results[3]))
```

```python
import jax
import jax.numpy as jnp
from jax import lax
from jax.experimental import pallas as pl
from jax.experimental.pallas import tpu as pltpu
from jax.sharding import PartitionSpec as P

HEADS = 32
HD = 128
MAX_LEN = 2560
SHARDS = 32
ROWS = MAX_LEN // SHARDS
TQ = 256
TK = 512
COLS = 8
LOG2E = 1.4426950408889634
SCALE = HD ** (-0.5)


def pack_body(q_ref, k_ref, v_ref, g_ref, out_ref):
    for number, ref in enumerate((q_ref, k_ref, v_ref, g_ref)):
        for h in range(COLS):
            out_ref[h, number] = ref[0, 0, :, h * HD : (h + 1) * HD]


def pack(arrays, video):
    spec = pl.BlockSpec((1, 1, ROWS, COLS * HD), lambda j: (0, video, 0, j))
    return pl.pallas_call(
        pack_body,
        grid=(HEADS // COLS,),
        in_specs=[spec] * 4,
        out_specs=pl.BlockSpec((COLS, 4, ROWS, HD), lambda j: (j, 0, 0, 0)),
        out_shape=jax.ShapeDtypeStruct((HEADS, 4, ROWS, HD), jnp.bfloat16),
        cost_estimate=pl.CostEstimate(flops=0, transcendentals=0, bytes_accessed=5242880),
        name=f"pack{video}",
    )(*arrays)


def unpack_body(in_ref, *refs):
    for number, ref in enumerate(refs[-4:]):
        for h in range(COLS):
            ref[0, 0, :, h * HD : (h + 1) * HD] = in_ref[h, number]


def unpack(back, video, earlier):
    spec = pl.BlockSpec((1, 1, ROWS, COLS * HD), lambda j: (0, video, 0, j))
    extra = [pl.BlockSpec(memory_space=pl.ANY)] * len(earlier)
    return pl.pallas_call(
        unpack_body,
        grid=(HEADS // COLS,),
        in_specs=[pl.BlockSpec((COLS, 4, ROWS, HD), lambda j: (j, 0, 0, 0))] + extra,
        out_specs=[spec] * 4,
        out_shape=[jax.ShapeDtypeStruct((1, 2, ROWS, HEADS * HD), jnp.bfloat16)] * 4,
        input_output_aliases={1 + i: i for i in range(len(earlier))},
        cost_estimate=pl.CostEstimate(flops=0, transcendentals=0, bytes_accessed=5242880),
        name=f"unpack{video}",
    )(back, *earlier)


def dot(a, b, dims):
    return lax.dot_general(a, b, (dims, ((), ())), preferred_element_type=jnp.float32)


def attend_body(
    len_ref, x_ref, out_ref, q_s, k_s, v_s, g_s, o_s, dq_s, s_s, w_s, dk_s, dv_s, m_s, l_s, acc_s
):
    length = len_ref[0]
    for s in range(SHARDS):
        rows = slice(s * ROWS, (s + 1) * ROWS)
        q_s[rows] = x_ref[s, 0]
        k_s[rows] = x_ref[s, 1]
        v_s[rows] = x_ref[s, 2]
        valid = lax.broadcasted_iota(jnp.int32, (ROWS, HD), 0) < length - s * ROWS
        g_s[rows] = jnp.where(valid, x_ref[s, 3].astype(jnp.float32), 0.0).astype(jnp.bfloat16)
    o_s[...] = jnp.zeros_like(o_s)
    dq_s[...] = jnp.zeros_like(dq_s)
    dk_s[...] = jnp.zeros_like(dk_s)
    dv_s[...] = jnp.zeros_like(dv_s)
    query_tiles = (length + TQ - 1) // TQ
    key_tiles = (length + TK - 1) // TK
    fold = SCALE * LOG2E

    def query_tile(i, _):
        r0 = pl.multiple_of(i * TQ, TQ)
        m_s[...] = jnp.full_like(m_s, -3.0e38)
        l_s[...] = jnp.zeros_like(l_s)
        acc_s[...] = jnp.zeros_like(acc_s)

        def score_pass(j, _):
            k0 = pl.multiple_of(j * TK, TK)
            s = dot(q_s[pl.ds(r0, TQ)], k_s[pl.ds(k0, TK)], ((1,), (1,)))
            col = lax.broadcasted_iota(jnp.int32, (1, TK), 1) + k0
            s = jnp.where(col < length, s, -1e30)
            s_s[:, pl.ds(k0, TK)] = s
            top = m_s[...]
            for c in range(TK // HD):
                top = jnp.maximum(top, s[:, c * HD : (c + 1) * HD])
            m_s[...] = top
            return 0

        lax.fori_loop(0, key_tiles, score_pass, 0)
        shift = jnp.max(m_s[...], axis=1, keepdims=True) * fold

        def weight_pass(j, _):
            k0 = pl.multiple_of(j * TK, TK)
            w = jnp.exp2(s_s[:, pl.ds(k0, TK)] * fold - shift)
            total = l_s[...]
            for c in range(TK // HD):
                total = total + w[:, c * HD : (c + 1) * HD]
            l_s[...] = total
            w = w.astype(jnp.bfloat16)
            w_s[:, pl.ds(k0, TK)] = w
            acc_s[...] += dot(w, v_s[pl.ds(k0, TK)], ((1,), (0,)))
            return 0

        lax.fori_loop(0, key_tiles, weight_pass, 0)
        inverse = 1.0 / jnp.sum(l_s[...], axis=1, keepdims=True)
        row = lax.broadcasted_iota(jnp.int32, (TQ, 1), 0) + r0
        output = jnp.where(row < length, acc_s[...] * inverse, 0.0).astype(jnp.bfloat16)
        o_s[pl.ds(r0, TQ)] = output
        delta = jnp.sum(
            g_s[pl.ds(r0, TQ)].astype(jnp.float32) * output.astype(jnp.float32),
            axis=1,
            keepdims=True,
        )
        acc_s[...] = jnp.zeros_like(acc_s)

        def grad_pass(j, _):
            k0 = pl.multiple_of(j * TK, TK)
            q = q_s[pl.ds(r0, TQ)]
            g = g_s[pl.ds(r0, TQ)]
            p = w_s[:, pl.ds(k0, TK)].astype(jnp.float32) * inverse
            dp = dot(g, v_s[pl.ds(k0, TK)], ((1,), (1,)))
            ds = (p * (dp - delta)).astype(jnp.bfloat16)
            acc_s[...] += dot(ds, k_s[pl.ds(k0, TK)], ((1,), (0,)))
            dk_s[pl.ds(k0, TK)] += dot(ds, q, ((0,), (0,)))
            dv_s[pl.ds(k0, TK)] += dot(p.astype(jnp.bfloat16), g, ((0,), (0,)))
            return 0

        lax.fori_loop(0, key_tiles, grad_pass, 0)
        dq_s[pl.ds(r0, TQ)] = (acc_s[...] * SCALE).astype(jnp.bfloat16)
        return 0

    lax.fori_loop(0, query_tiles, query_tile, 0)
    for s in range(SHARDS):
        rows = slice(s * ROWS, (s + 1) * ROWS)
        out_ref[s, 0] = o_s[rows]
        out_ref[s, 1] = dq_s[rows]
        out_ref[s, 2] = (dk_s[rows] * SCALE).astype(jnp.bfloat16)
        out_ref[s, 3] = dv_s[rows].astype(jnp.bfloat16)


def attend(length, received, video):
    half = pltpu.VMEM((MAX_LEN, HD), jnp.bfloat16)
    full = pltpu.VMEM((MAX_LEN, HD), jnp.float32)
    tile = pltpu.VMEM((TQ, HD), jnp.float32)
    return pl.pallas_call(
        attend_body,
        in_specs=[
            pl.BlockSpec(memory_space=pltpu.SMEM),
            pl.BlockSpec(memory_space=pltpu.VMEM),
        ],
        out_specs=pl.BlockSpec(memory_space=pltpu.VMEM),
        out_shape=jax.ShapeDtypeStruct((SHARDS, 4, ROWS, HD), jnp.bfloat16),
        scratch_shapes=[half] * 6
        + [
            pltpu.VMEM((TQ, MAX_LEN), jnp.float32),
            pltpu.VMEM((TQ, MAX_LEN), jnp.bfloat16),
            full,
            full,
            tile,
            tile,
            tile,
        ],
        compiler_params=pltpu.CompilerParams(vmem_limit_bytes=32 * 1024 * 1024),
        cost_estimate=pl.CostEstimate(
            flops=10 * MAX_LEN * MAX_LEN * HD,
            transcendentals=MAX_LEN * MAX_LEN,
            bytes_accessed=5242880,
        ),
        name=f"attend{video}",
    )(length, received)


def exchange(value):
    return lax.all_to_all(value, "seq", split_axis=0, concat_axis=0, tiled=True)


def per_device(query_rows, key_rows, value_rows, out_grad, lengths):
    arrays = (query_rows, key_rows, value_rows, out_grad)
    own = lax.dynamic_index_in_dim(lengths, lax.axis_index("grp"), 0, keepdims=False)
    outputs = ()
    for video in range(2):
        received = exchange(pack(arrays, video))
        computed = attend(own[video : video + 1], received, video)
        outputs = unpack(exchange(computed), video, outputs)
    return tuple(outputs)


def solution(mesh):
    rows = P("grp", None, "seq", None)
    return jax.shard_map(
        per_device,
        mesh=mesh,
        in_specs=(rows, rows, rows, rows, P()),
        out_specs=(rows, rows, rows, rows),
        check_vma=False,
    )
```

```python
import jax
import jax.numpy as jnp
from jax import lax
from jax.experimental import pallas as pl
from jax.experimental.pallas import tpu as pltpu
from jax.sharding import PartitionSpec as P

HEADS = 32
HD = 128
MAX_LEN = 2560
SHARDS = 32
ROWS = MAX_LEN // SHARDS
TQ = 512
TK = 2560
STAGGER = 25000
COLS = 16
LOG2E = 1.4426950408889634
SCALE = HD ** (-0.5)


def pack_body(wait_ref, q_ref, k_ref, v_ref, g_ref, out_ref):
    @pl.when(jnp.logical_and(pl.program_id(0) == 0, wait_ref[0] == 1))
    def _():
        pl.delay(STAGGER)

    for number, ref in enumerate((q_ref, k_ref, v_ref, g_ref)):
        for h in range(COLS):
            out_ref[h, number] = ref[0, 0, :, h * HD : (h + 1) * HD]


def pack(late, arrays, video):
    spec = pl.BlockSpec((1, 1, ROWS, COLS * HD), lambda j: (0, video, 0, j))
    return pl.pallas_call(
        pack_body,
        grid=(HEADS // COLS,),
        in_specs=[pl.BlockSpec(memory_space=pltpu.SMEM)] + [spec] * 4,
        out_specs=pl.BlockSpec((COLS, 4, ROWS, HD), lambda j: (j, 0, 0, 0)),
        out_shape=jax.ShapeDtypeStruct((HEADS, 4, ROWS, HD), jnp.bfloat16),
        cost_estimate=pl.CostEstimate(flops=0, transcendentals=0, bytes_accessed=5242880),
        name=f"pack{video}",
    )(late, *arrays)


def unpack_body(in_ref, *refs):
    for number, ref in enumerate(refs[-4:]):
        for h in range(COLS):
            ref[0, 0, :, h * HD : (h + 1) * HD] = in_ref[h, number]


def unpack(back, video, earlier):
    spec = pl.BlockSpec((1, 1, ROWS, COLS * HD), lambda j: (0, video, 0, j))
    extra = [pl.BlockSpec(memory_space=pl.ANY)] * len(earlier)
    return pl.pallas_call(
        unpack_body,
        grid=(HEADS // COLS,),
        in_specs=[pl.BlockSpec((COLS, 4, ROWS, HD), lambda j: (j, 0, 0, 0))] + extra,
        out_specs=[spec] * 4,
        out_shape=[jax.ShapeDtypeStruct((1, 2, ROWS, HEADS * HD), jnp.bfloat16)] * 4,
        input_output_aliases={1 + i: i for i in range(len(earlier))},
        cost_estimate=pl.CostEstimate(flops=0, transcendentals=0, bytes_accessed=5242880),
        name=f"unpack{video}",
    )(back, *earlier)


def dot(a, b, dims):
    return lax.dot_general(a, b, (dims, ((), ())), preferred_element_type=jnp.float32)


def attend_body(
    len_ref, x_hbm, out_hbm, x_ref, q_s, k_s, v_s, g_s, o_s, dq_s, s_s, w_s, dk_s, dv_s, m_s, l_s,
    acc_s, sem
):
    length = len_ref[0]
    load = pltpu.make_async_copy(x_hbm, x_ref, sem)
    load.start()
    load.wait()
    for s in range(SHARDS):
        rows = slice(s * ROWS, (s + 1) * ROWS)
        q_s[rows] = x_ref[s, 0]
        k_s[rows] = x_ref[s, 1]
        v_s[rows] = x_ref[s, 2]
        valid = lax.broadcasted_iota(jnp.int32, (ROWS, HD), 0) < length - s * ROWS
        g_s[rows] = jnp.where(valid, x_ref[s, 3].astype(jnp.float32), 0.0).astype(jnp.bfloat16)
    o_s[...] = jnp.zeros_like(o_s)
    dq_s[...] = jnp.zeros_like(dq_s)
    dk_s[...] = jnp.zeros_like(dk_s)
    dv_s[...] = jnp.zeros_like(dv_s)
    query_tiles = (length + TQ - 1) // TQ
    key_tiles = (length + TK - 1) // TK
    fold = SCALE * LOG2E

    def query_tile(i, _):
        r0 = pl.multiple_of(i * TQ, TQ)
        m_s[...] = jnp.full_like(m_s, -3.0e38)
        l_s[...] = jnp.zeros_like(l_s)
        acc_s[...] = jnp.zeros_like(acc_s)

        def score_pass(j, _):
            k0 = pl.multiple_of(j * TK, TK)
            s = dot(q_s[pl.ds(r0, TQ)], k_s[pl.ds(k0, TK)], ((1,), (1,)))
            col = lax.broadcasted_iota(jnp.int32, (1, TK), 1) + k0
            s = jnp.where(col < length, s, -1e30)
            s_s[:, pl.ds(k0, TK)] = s
            top = m_s[...]
            for c in range(TK // HD):
                top = jnp.maximum(top, s[:, c * HD : (c + 1) * HD])
            m_s[...] = top
            return 0

        lax.fori_loop(0, key_tiles, score_pass, 0)
        shift = jnp.max(m_s[...], axis=1, keepdims=True) * fold

        def weight_pass(j, _):
            k0 = pl.multiple_of(j * TK, TK)
            w = jnp.exp2(s_s[:, pl.ds(k0, TK)] * fold - shift)
            total = l_s[...]
            for c in range(TK // HD):
                total = total + w[:, c * HD : (c + 1) * HD]
            l_s[...] = total
            w = w.astype(jnp.bfloat16)
            w_s[:, pl.ds(k0, TK)] = w
            acc_s[...] += dot(w, v_s[pl.ds(k0, TK)], ((1,), (0,)))
            return 0

        lax.fori_loop(0, key_tiles, weight_pass, 0)
        inverse = 1.0 / jnp.sum(l_s[...], axis=1, keepdims=True)
        row = lax.broadcasted_iota(jnp.int32, (TQ, 1), 0) + r0
        output = jnp.where(row < length, acc_s[...] * inverse, 0.0).astype(jnp.bfloat16)
        o_s[pl.ds(r0, TQ)] = output
        delta = jnp.sum(
            g_s[pl.ds(r0, TQ)].astype(jnp.float32) * output.astype(jnp.float32),
            axis=1,
            keepdims=True,
        )
        acc_s[...] = jnp.zeros_like(acc_s)

        def grad_pass(j, _):
            k0 = pl.multiple_of(j * TK, TK)
            q = q_s[pl.ds(r0, TQ)]
            g = g_s[pl.ds(r0, TQ)]
            p = w_s[:, pl.ds(k0, TK)].astype(jnp.float32) * inverse
            dp = dot(g, v_s[pl.ds(k0, TK)], ((1,), (1,)))
            ds = (p * (dp - delta)).astype(jnp.bfloat16)
            acc_s[...] += dot(ds, k_s[pl.ds(k0, TK)], ((1,), (0,)))
            dk_s[pl.ds(k0, TK)] += dot(ds, q, ((0,), (0,)))
            dv_s[pl.ds(k0, TK)] += dot(p.astype(jnp.bfloat16), g, ((0,), (0,)))
            return 0

        lax.fori_loop(0, key_tiles, grad_pass, 0)
        dq_s[pl.ds(r0, TQ)] = (acc_s[...] * SCALE).astype(jnp.bfloat16)
        return 0

    lax.fori_loop(0, query_tiles, query_tile, 0)
    for s in range(SHARDS):
        rows = slice(s * ROWS, (s + 1) * ROWS)
        x_ref[s, 0] = o_s[rows]
        x_ref[s, 1] = dq_s[rows]
        x_ref[s, 2] = (dk_s[rows] * SCALE).astype(jnp.bfloat16)
        x_ref[s, 3] = dv_s[rows].astype(jnp.bfloat16)
    store = pltpu.make_async_copy(x_ref, out_hbm, sem)
    store.start()
    store.wait()


def attend(length, received, video):
    half = pltpu.VMEM((MAX_LEN, HD), jnp.bfloat16)
    full = pltpu.VMEM((MAX_LEN, HD), jnp.float32)
    tile = pltpu.VMEM((TQ, HD), jnp.float32)
    return pl.pallas_call(
        attend_body,
        in_specs=[
            pl.BlockSpec(memory_space=pltpu.SMEM),
            pl.BlockSpec(memory_space=pltpu.HBM),
        ],
        out_specs=pl.BlockSpec(memory_space=pltpu.HBM),
        out_shape=jax.ShapeDtypeStruct((SHARDS, 4, ROWS, HD), jnp.bfloat16),
        scratch_shapes=[pltpu.VMEM((SHARDS, 4, ROWS, HD), jnp.bfloat16)]
        + [half] * 6
        + [
            pltpu.VMEM((TQ, MAX_LEN), jnp.float32),
            pltpu.VMEM((TQ, MAX_LEN), jnp.bfloat16),
            full,
            full,
            tile,
            tile,
            tile,
            pltpu.SemaphoreType.DMA,
        ],
        cost_estimate=pl.CostEstimate(
            flops=10 * MAX_LEN * MAX_LEN * HD,
            transcendentals=MAX_LEN * MAX_LEN,
            bytes_accessed=5242880,
        ),
        name=f"attend{video}",
    )(length, received)


def exchange(value):
    return lax.all_to_all(value, "seq", split_axis=0, concat_axis=0, tiled=True)


def per_device(query_rows, key_rows, value_rows, out_grad, lengths):
    arrays = (query_rows, key_rows, value_rows, out_grad)
    group = lax.axis_index("grp")
    own = lax.dynamic_index_in_dim(lengths, group, 0, keepdims=False)
    late = (group % 2).reshape(1)
    outputs = ()
    for video in range(2):
        received = exchange(pack(late * (1 - video), arrays, video))
        computed = attend(own[video : video + 1], received, video)
        outputs = unpack(exchange(computed), video, outputs)
    return tuple(outputs)


def solution(mesh):
    rows = P("grp", None, "seq", None)
    return jax.shard_map(
        per_device,
        mesh=mesh,
        in_specs=(rows, rows, rows, rows, P()),
        out_specs=(rows, rows, rows, rows),
        check_vma=False,
    )
```

```python
import functools

import jax
import jax.numpy as jnp
from jax import lax
from jax.experimental import pallas as pl
from jax.experimental.pallas import tpu as pltpu
from jax.sharding import PartitionSpec as P

HEADS = 32
HD = 128
MAX_LEN = 2560
SHARDS = 32
ROWS = MAX_LEN // SHARDS
TILE = 512
STAGGER = 24000
PARTS = 2
LOG2E = 1.4426950408889634
SCALE = HD ** (-0.5)


def pack_body(video, late_ref, q_ref, k_ref, v_ref, g_ref, out_ref, rows, held, in_sem, out_sem):
    @pl.when(late_ref[0] == 1)
    def _():
        pl.delay(STAGGER)

    wide = HEADS // PARTS
    pieces = [(a, p) for a in range(4) for p in range(PARTS)]
    refs = (q_ref, k_ref, v_ref, g_ref)

    def load(a, p):
        columns = slice(p * wide * HD, (p + 1) * wide * HD)
        return pltpu.make_async_copy(
            refs[a].at[0, video, :, columns], rows.at[a, :, columns], in_sem.at[a, p]
        )

    def store(a, p):
        heads = slice(p * wide, (p + 1) * wide)
        return pltpu.make_async_copy(held.at[heads, a], out_ref.at[heads, a], out_sem.at[a, p])

    for piece in pieces:
        load(*piece).start()
    for a, p in pieces:
        load(a, p).wait()
        for h in range(p * wide, (p + 1) * wide):
            held[h, a] = rows[a, :, h * HD : (h + 1) * HD]
        store(a, p).start()
    for piece in pieces:
        store(*piece).wait()


def pack(late, arrays, video):
    hbm = pl.BlockSpec(memory_space=pltpu.HBM)
    return pl.pallas_call(
        functools.partial(pack_body, video),
        in_specs=[pl.BlockSpec(memory_space=pltpu.SMEM)] + [hbm] * 4,
        out_specs=hbm,
        out_shape=jax.ShapeDtypeStruct((HEADS, 4, ROWS, HD), jnp.bfloat16),
        scratch_shapes=[
            pltpu.VMEM((4, ROWS, HEADS * HD), jnp.bfloat16),
            pltpu.VMEM((HEADS, 4, ROWS, HD), jnp.bfloat16),
            pltpu.SemaphoreType.DMA((4, PARTS)),
            pltpu.SemaphoreType.DMA((4, PARTS)),
        ],
        cost_estimate=pl.CostEstimate(flops=0, transcendentals=0, bytes_accessed=5242880),
        name=f"pack{video}",
    )(late, *arrays)


def unpack_body(video, count, in_ref, *refs):
    outs, (held, rows, in_sem, out_sem) = refs[count : count + 4], refs[count + 4 :]
    wide = HEADS // PARTS
    pieces = [(a, p) for a in range(4) for p in range(PARTS)]

    def load(a, p):
        heads = slice(p * wide, (p + 1) * wide)
        return pltpu.make_async_copy(in_ref.at[heads, a], held.at[heads, a], in_sem.at[a, p])

    def store(a, p):
        columns = slice(p * wide * HD, (p + 1) * wide * HD)
        return pltpu.make_async_copy(
            rows.at[a, :, columns], outs[a].at[0, video, :, columns], out_sem.at[a, p]
        )

    for piece in pieces:
        load(*piece).start()
    for a, p in pieces:
        load(a, p).wait()
        for h in range(p * wide, (p + 1) * wide):
            rows[a, :, h * HD : (h + 1) * HD] = held[h, a]
        store(a, p).start()
    for piece in pieces:
        store(*piece).wait()


def unpack(back, video, earlier):
    hbm = pl.BlockSpec(memory_space=pltpu.HBM)
    return pl.pallas_call(
        functools.partial(unpack_body, video, len(earlier)),
        in_specs=[hbm] * (1 + len(earlier)),
        out_specs=[hbm] * 4,
        out_shape=[jax.ShapeDtypeStruct((1, 2, ROWS, HEADS * HD), jnp.bfloat16)] * 4,
        input_output_aliases={1 + i: i for i in range(len(earlier))},
        scratch_shapes=[
            pltpu.VMEM((HEADS, 4, ROWS, HD), jnp.bfloat16),
            pltpu.VMEM((4, ROWS, HEADS * HD), jnp.bfloat16),
            pltpu.SemaphoreType.DMA((4, PARTS)),
            pltpu.SemaphoreType.DMA((4, PARTS)),
        ],
        cost_estimate=pl.CostEstimate(flops=0, transcendentals=0, bytes_accessed=5242880),
        name=f"unpack{video}",
    )(back, *earlier)


def dot(a, b, dims):
    return lax.dot_general(a, b, (dims, ((), ())), preferred_element_type=jnp.float32)


def attend_body(
    len_ref, x_hbm, out_hbm, x_ref, q_s, k_s, v_s, g_s, o_s, dq_s, dk_s, dv_s, sem
):
    length = len_ref[0]
    load = pltpu.make_async_copy(x_hbm, x_ref, sem)
    load.start()
    load.wait()

    def bring(s, _):
        start = pl.multiple_of(s * ROWS, ROWS)
        rows = pl.ds(start, ROWS)
        q_s[rows] = x_ref[s, 0]
        k_s[rows] = x_ref[s, 1]
        v_s[rows] = x_ref[s, 2]
        valid = lax.broadcasted_iota(jnp.int32, (ROWS, HD), 0) < length - start
        g_s[rows] = jnp.where(valid, x_ref[s, 3].astype(jnp.float32), 0.0).astype(jnp.bfloat16)
        return 0

    lax.fori_loop(0, SHARDS, bring, 0)
    o_s[...] = jnp.zeros_like(o_s)
    dq_s[...] = jnp.zeros_like(dq_s)
    dk_s[...] = jnp.zeros_like(dk_s)
    dv_s[...] = jnp.zeros_like(dv_s)
    fold = SCALE * LOG2E

    def query_tile(i, _):
        here = pl.ds(pl.multiple_of(i * TILE, TILE), TILE)
        s = dot(q_s[here], k_s[...], ((1,), (1,)))
        col = lax.broadcasted_iota(jnp.int32, (1, MAX_LEN), 1)
        s = jnp.where(col < length, s, -1e30)
        shift = jnp.max(s, axis=1, keepdims=True) * fold
        w = jnp.exp2(s * fold - shift)
        inverse = 1.0 / jnp.sum(w, axis=1, keepdims=True)
        w = w.astype(jnp.bfloat16)
        row = lax.broadcasted_iota(jnp.int32, (TILE, 1), 0) + i * TILE
        output = dot(w, v_s[...], ((1,), (0,))) * inverse
        output = jnp.where(row < length, output, 0.0).astype(jnp.bfloat16)
        o_s[here] = output
        g = g_s[here]
        delta = jnp.sum(
            g.astype(jnp.float32) * output.astype(jnp.float32), axis=1, keepdims=True
        )
        p = w.astype(jnp.float32) * inverse
        dv_s[...] += dot(p.astype(jnp.bfloat16), g, ((0,), (0,)))
        dp = dot(g, v_s[...], ((1,), (1,)))
        ds = (p * (dp - delta)).astype(jnp.bfloat16)
        dq_s[here] = (dot(ds, k_s[...], ((1,), (0,))) * SCALE).astype(jnp.bfloat16)
        dk_s[...] += dot(ds, q_s[here], ((0,), (0,)))
        return 0

    lax.fori_loop(0, (length + TILE - 1) // TILE, query_tile, 0)

    def give(s, _):
        rows = pl.ds(pl.multiple_of(s * ROWS, ROWS), ROWS)
        x_ref[s, 0] = o_s[rows]
        x_ref[s, 1] = dq_s[rows]
        x_ref[s, 2] = (dk_s[rows] * SCALE).astype(jnp.bfloat16)
        x_ref[s, 3] = dv_s[rows].astype(jnp.bfloat16)
        return 0

    lax.fori_loop(0, SHARDS, give, 0)
    store = pltpu.make_async_copy(x_ref, out_hbm, sem)
    store.start()
    store.wait()


def attend(length, received, video):
    half = pltpu.VMEM((MAX_LEN, HD), jnp.bfloat16)
    full = pltpu.VMEM((MAX_LEN, HD), jnp.float32)
    hbm = pl.BlockSpec(memory_space=pltpu.HBM)
    return pl.pallas_call(
        attend_body,
        in_specs=[pl.BlockSpec(memory_space=pltpu.SMEM), hbm],
        out_specs=hbm,
        out_shape=jax.ShapeDtypeStruct(received.shape, jnp.bfloat16),
        scratch_shapes=[pltpu.VMEM(received.shape, jnp.bfloat16)]
        + [half] * 6
        + [full, full, pltpu.SemaphoreType.DMA],
        cost_estimate=pl.CostEstimate(
            flops=10 * MAX_LEN * MAX_LEN * HD,
            transcendentals=MAX_LEN * MAX_LEN,
            bytes_accessed=4 * MAX_LEN * HD * 4,
        ),
        name=f"attend{video}",
    )(length, received)


def exchange(value):
    return lax.all_to_all(value, "seq", split_axis=0, concat_axis=0, tiled=True)


def per_device(query_rows, key_rows, value_rows, out_grad, lengths):
    arrays = (query_rows, key_rows, value_rows, out_grad)
    group = lax.axis_index("grp")
    own = lax.dynamic_index_in_dim(lengths, group, 0, keepdims=False)
    late = (group % 2).reshape(1)
    outputs = ()
    for video in range(2):
        received = exchange(pack(late * (1 - video), arrays, video))
        computed = attend(own[video : video + 1], received, video)
        outputs = unpack(exchange(computed), video, outputs)
    return tuple(outputs)


def solution(mesh):
    rows = P("grp", None, "seq", None)
    return jax.shard_map(
        per_device,
        mesh=mesh,
        in_specs=(rows, rows, rows, rows, P()),
        out_specs=(rows, rows, rows, rows),
        check_vma=False,
    )
```

```python
import functools

import jax
import jax.numpy as jnp
from jax import lax
from jax.experimental import pallas as pl
from jax.experimental.pallas import tpu as pltpu
from jax.sharding import PartitionSpec as P

HEADS = 32
HD = 128
MAX_LEN = 2560
SHARDS = 32
ROWS = MAX_LEN // SHARDS
TILE = 512
STAGGER = 24000
PARTS = 2
VMEM = 67043328
LOG2E = 1.4426950408889634
SCALE = HD ** (-0.5)


def pack_body(video, late_ref, q_ref, k_ref, v_ref, g_ref, out_ref, rows, held, in_sem, out_sem):
    @pl.when(late_ref[0] == 1)
    def _():
        pl.delay(STAGGER)

    wide = HEADS // PARTS
    pieces = [(a, p) for a in range(4) for p in range(PARTS)]
    refs = (q_ref, k_ref, v_ref, g_ref)

    def load(a, p):
        columns = slice(p * wide * HD, (p + 1) * wide * HD)
        return pltpu.make_async_copy(
            refs[a].at[0, video, :, columns], rows.at[a, :, columns], in_sem.at[a, p]
        )

    def store(a, p):
        heads = slice(p * wide, (p + 1) * wide)
        return pltpu.make_async_copy(held.at[heads, a], out_ref.at[heads, a], out_sem.at[a, p])

    for piece in pieces:
        load(*piece).start()
    for a, p in pieces:
        load(a, p).wait()
        for h in range(p * wide, (p + 1) * wide):
            held[h, a] = rows[a, :, h * HD : (h + 1) * HD]
        store(a, p).start()
    for piece in pieces:
        store(*piece).wait()


def pack(late, arrays, video):
    hbm = pl.BlockSpec(memory_space=pltpu.HBM)
    return pl.pallas_call(
        functools.partial(pack_body, video),
        in_specs=[pl.BlockSpec(memory_space=pltpu.SMEM)] + [hbm] * 4,
        out_specs=hbm,
        out_shape=jax.ShapeDtypeStruct((HEADS, 4, ROWS, HD), jnp.bfloat16),
        scratch_shapes=[
            pltpu.VMEM((4, ROWS, HEADS * HD), jnp.bfloat16),
            pltpu.VMEM((HEADS, 4, ROWS, HD), jnp.bfloat16),
            pltpu.SemaphoreType.DMA((4, PARTS)),
            pltpu.SemaphoreType.DMA((4, PARTS)),
        ],
        compiler_params=pltpu.CompilerParams(vmem_limit_bytes=VMEM),
        cost_estimate=pl.CostEstimate(flops=0, transcendentals=0, bytes_accessed=5242880),
        name=f"pack{video}",
    )(late, *arrays)


def unpack_body(video, count, in_ref, *refs):
    outs, (held, rows, in_sem, out_sem) = refs[count : count + 4], refs[count + 4 :]
    wide = HEADS // PARTS
    pieces = [(a, p) for a in range(4) for p in range(PARTS)]

    def load(a, p):
        heads = slice(p * wide, (p + 1) * wide)
        return pltpu.make_async_copy(in_ref.at[heads, a], held.at[heads, a], in_sem.at[a, p])

    def store(a, p):
        columns = slice(p * wide * HD, (p + 1) * wide * HD)
        return pltpu.make_async_copy(
            rows.at[a, :, columns], outs[a].at[0, video, :, columns], out_sem.at[a, p]
        )

    for piece in pieces:
        load(*piece).start()
    for a, p in pieces:
        load(a, p).wait()
        for h in range(p * wide, (p + 1) * wide):
            rows[a, :, h * HD : (h + 1) * HD] = held[h, a]
        store(a, p).start()
    for piece in pieces:
        store(*piece).wait()


def unpack(back, video, earlier):
    hbm = pl.BlockSpec(memory_space=pltpu.HBM)
    return pl.pallas_call(
        functools.partial(unpack_body, video, len(earlier)),
        in_specs=[hbm] * (1 + len(earlier)),
        out_specs=[hbm] * 4,
        out_shape=[jax.ShapeDtypeStruct((1, 2, ROWS, HEADS * HD), jnp.bfloat16)] * 4,
        input_output_aliases={1 + i: i for i in range(len(earlier))},
        scratch_shapes=[
            pltpu.VMEM((HEADS, 4, ROWS, HD), jnp.bfloat16),
            pltpu.VMEM((4, ROWS, HEADS * HD), jnp.bfloat16),
            pltpu.SemaphoreType.DMA((4, PARTS)),
            pltpu.SemaphoreType.DMA((4, PARTS)),
        ],
        compiler_params=pltpu.CompilerParams(vmem_limit_bytes=VMEM),
        cost_estimate=pl.CostEstimate(flops=0, transcendentals=0, bytes_accessed=5242880),
        name=f"unpack{video}",
    )(back, *earlier)


def dot(a, b, dims):
    return lax.dot_general(a, b, (dims, ((), ())), preferred_element_type=jnp.float32)


def attend_body(
    len_ref, x_hbm, out_hbm, x_ref, q_s, k_s, v_s, g_s, o_s, dq_s, dk_s, dv_s, sem
):
    length = len_ref[0]
    load = pltpu.make_async_copy(x_hbm, x_ref, sem)
    load.start()
    load.wait()

    def bring(s, _):
        start = pl.multiple_of(s * ROWS, ROWS)
        rows = pl.ds(start, ROWS)
        q_s[rows] = x_ref[s, 0]
        k_s[rows] = x_ref[s, 1]
        v_s[rows] = x_ref[s, 2]
        valid = lax.broadcasted_iota(jnp.int32, (ROWS, HD), 0) < length - start
        g_s[rows] = jnp.where(valid, x_ref[s, 3].astype(jnp.float32), 0.0).astype(jnp.bfloat16)
        return 0

    lax.fori_loop(0, SHARDS, bring, 0)
    o_s[...] = jnp.zeros_like(o_s)
    dq_s[...] = jnp.zeros_like(dq_s)
    dk_s[...] = jnp.zeros_like(dk_s)
    dv_s[...] = jnp.zeros_like(dv_s)
    fold = SCALE * LOG2E

    def query_tile(i, _):
        here = pl.ds(pl.multiple_of(i * TILE, TILE), TILE)
        s = dot(q_s[here], k_s[...], ((1,), (1,)))
        col = lax.broadcasted_iota(jnp.int32, (1, MAX_LEN), 1)
        s = jnp.where(col < length, s, -1e30)
        shift = jnp.max(s, axis=1, keepdims=True) * fold
        w = jnp.exp2(s * fold - shift)
        inverse = 1.0 / jnp.sum(w, axis=1, keepdims=True)
        w = w.astype(jnp.bfloat16)
        row = lax.broadcasted_iota(jnp.int32, (TILE, 1), 0) + i * TILE
        output = dot(w, v_s[...], ((1,), (0,))) * inverse
        output = jnp.where(row < length, output, 0.0).astype(jnp.bfloat16)
        o_s[here] = output
        g = g_s[here]
        delta = jnp.sum(
            g.astype(jnp.float32) * output.astype(jnp.float32), axis=1, keepdims=True
        )
        p = w.astype(jnp.float32) * inverse
        dv_s[...] += dot(p.astype(jnp.bfloat16), g, ((0,), (0,)))
        dp = dot(g, v_s[...], ((1,), (1,)))
        ds = (p * (dp - delta)).astype(jnp.bfloat16)
        dq_s[here] = (dot(ds, k_s[...], ((1,), (0,))) * SCALE).astype(jnp.bfloat16)
        dk_s[...] += dot(ds, q_s[here], ((0,), (0,)))
        return 0

    lax.fori_loop(0, (length + TILE - 1) // TILE, query_tile, 0)

    def give(s, _):
        rows = pl.ds(pl.multiple_of(s * ROWS, ROWS), ROWS)
        x_ref[s, 0] = o_s[rows]
        x_ref[s, 1] = dq_s[rows]
        x_ref[s, 2] = (dk_s[rows] * SCALE).astype(jnp.bfloat16)
        x_ref[s, 3] = dv_s[rows].astype(jnp.bfloat16)
        return 0

    lax.fori_loop(0, SHARDS, give, 0)
    store = pltpu.make_async_copy(x_ref, out_hbm, sem)
    store.start()
    store.wait()


def attend(length, received, video):
    half = pltpu.VMEM((MAX_LEN, HD), jnp.bfloat16)
    full = pltpu.VMEM((MAX_LEN, HD), jnp.float32)
    hbm = pl.BlockSpec(memory_space=pltpu.HBM)
    return pl.pallas_call(
        attend_body,
        in_specs=[pl.BlockSpec(memory_space=pltpu.SMEM), hbm],
        out_specs=hbm,
        out_shape=jax.ShapeDtypeStruct(received.shape, jnp.bfloat16),
        scratch_shapes=[pltpu.VMEM(received.shape, jnp.bfloat16)]
        + [half] * 6
        + [full, full, pltpu.SemaphoreType.DMA],
        compiler_params=pltpu.CompilerParams(vmem_limit_bytes=VMEM),
        cost_estimate=pl.CostEstimate(
            flops=10 * MAX_LEN * MAX_LEN * HD,
            transcendentals=MAX_LEN * MAX_LEN,
            bytes_accessed=4 * MAX_LEN * HD * 4,
        ),
        name=f"attend{video}",
    )(length, received)


def exchange(value):
    return lax.all_to_all(value, "seq", split_axis=0, concat_axis=0, tiled=True)


def per_device(query_rows, key_rows, value_rows, out_grad, lengths):
    arrays = (query_rows, key_rows, value_rows, out_grad)
    group = lax.axis_index("grp")
    own = lax.dynamic_index_in_dim(lengths, group, 0, keepdims=False)
    late = (group % 2).reshape(1)
    outputs = ()
    for video in range(2):
        received = exchange(pack(late * (1 - video), arrays, video))
        computed = attend(own[video : video + 1], received, video)
        outputs = unpack(exchange(computed), video, outputs)
    return tuple(outputs)


def solution(mesh):
    rows = P("grp", None, "seq", None)
    return jax.shard_map(
        per_device,
        mesh=mesh,
        in_specs=(rows, rows, rows, rows, P()),
        out_specs=(rows, rows, rows, rows),
        check_vma=False,
    )
```
